768 devices in a mesh: lat: 24 (over z, core), lon: 32 (over y, x).
Axes of the slice: x: 4, y: 8, z: 12, core: 2. Of those that a mesh axis runs over, the one named last changes fastest.
Arguments:
- queries: bfloat16 [48, 2048, 2048], P('lat', 'lon'), may hold values from -50 to 50
- keyval: bfloat16 [2, 48, 2048, 2048], P(None, 'lat', 'lon'), may hold values from -5 to 5
- keep: int32 [48], replicated, may hold values from 0 to 1, as said below
- lists: int32 [48, 64, 13], P('lat', 'lon'), may hold values from 0 to 14, as said below
Outputs:
- attended: bfloat16 [48, 2048, 2048], P('lat', 'lon')
- gram_factor: float32 [24, 16, 128, 128], P('lat')
The draws below stay inside these ranges and needn't reach their ends.
Inputs may be any that keep to these rules, and one draw needn't show every extreme that they name: `lists`: each list holds 13 different candidate numbers; its first is 7, the query block itself. keep is 0 in rows 0 and 47, and 1 outside the first and last 12 rows.
All inputs are finite; a program needn't handle non-finite values.
Results may differ from the reference program's by a relative error of at most 0.015.
Values may be sent and summed in bfloat16 or wider, within the bound.
No kernel may reach another device: no remote copies, remote signals or barrier semaphores. Data moves between devices by JAX's collectives and lax.ppermute only.
A program may use at most 64 MiB of HBM per device.

```python
import jax
import jax.numpy as jnp
from jax import lax

HEADS = 16
HD = 128
BLOCK = 32
HALO = 2
NB = 13
TLAT = 2
CAND = 15
NLAT = 48
NLON = 2048
NBLK = 64
POLAR = 12
N_LAT = 24


def field_shape():
    return (NLAT, NLON, HEADS * HD)


def unit_normal(key, shape):
    return jnp.clip(jax.random.normal(key, shape, jnp.float32), -5.0, 5.0)


def draw_queries(key, part):
    return unit_normal(jax.random.fold_in(key, 3), field_shape()).astype(jnp.bfloat16)


def draw_keyval(key, part):
    keys_f = unit_normal(jax.random.fold_in(key, 1), field_shape())
    values_f = unit_normal(jax.random.fold_in(key, 2), field_shape())
    return jnp.stack([keys_f, values_f], 0).astype(jnp.bfloat16)


def draw_keep(key, part):
    row_index = jnp.arange(NLAT)
    coin_flip = jax.random.randint(jax.random.fold_in(key, 21), (NLAT,), 0, 2)
    polar_cap = (row_index < POLAR) | (row_index >= NLAT - POLAR)
    pole_rows = (row_index == 0) | (row_index == NLAT - 1)
    return jnp.where(pole_rows, 0, jnp.where(polar_cap, coin_flip, 1)).astype(jnp.int32)


def draw_lists(key, part):
    list_count = NLAT * NBLK
    raw_scores = jax.random.randint(jax.random.fold_in(key, 31), (list_count, CAND - 1), 0, 1 << 20) * 16
    raw_scores = raw_scores + jnp.arange(CAND - 1, dtype=jnp.int32)[None, :]
    ordering = jnp.argsort(raw_scores, axis=1).astype(jnp.int32)
    own_block = 3 * HALO + 1
    others = ordering[:, :NB - 1]
    others = others + (others >= own_block).astype(jnp.int32)
    complete = jnp.concatenate([jnp.full((list_count, 1), own_block, jnp.int32), others], axis=1)
    return complete.reshape(NLAT, NBLK, NB).astype(jnp.int32)


def setup_inputs(seed: int = 0) -> dict:
    splits = jax.random.split(jax.random.key(seed), 5)
    return {
        "queries": draw_queries(jax.random.fold_in(splits[4], 71), 0),
        "keyval": draw_keyval(jax.random.fold_in(splits[4], 71), 0),
        "keep": draw_keep(jax.random.fold_in(splits[4], 71), 0),
        "lists": draw_lists(jax.random.fold_in(splits[4], 71), 0),
    }


def row_attention(lat_row, queries, keyval, keep, lists):
    block_count = NLON // BLOCK
    query_row = lax.dynamic_index_in_dim(queries, lat_row, 0, keepdims=False)
    candidates = []
    usable_rows = []
    for offset in range(2 * HALO + 1):
        source = lat_row + offset - HALO
        clamped = jnp.clip(source, 0, NLAT - 1).astype(jnp.int32)
        row_slab = lax.dynamic_index_in_dim(keyval, clamped, 1, keepdims=False)
        row_slab = row_slab.reshape(2, block_count, BLOCK, HEADS * HD)
        for lon_step in range(3):
            candidates.append(jnp.roll(row_slab, 1 - lon_step, axis=1))
        inside = (source >= 0) & (source < NLAT)
        seen = jnp.logical_or(offset == HALO, lax.dynamic_index_in_dim(keep, clamped, 0, keepdims=False) == 1)
        usable_rows.append(inside & seen)
    stacked = jnp.moveaxis(jnp.stack(candidates, 0), 2, 0)
    row_lists = lax.dynamic_index_in_dim(lists, lat_row, 0, keepdims=False)
    chosen = jnp.take_along_axis(stacked, row_lists[:, :, None, None, None], axis=1)
    usable = jnp.stack(usable_rows, 0)[row_lists // 3]
    key_part = chosen[:, :, 0].reshape(block_count, NB * BLOCK, HEADS, HD).astype(jnp.float32)
    value_part = chosen[:, :, 1].reshape(block_count, NB * BLOCK, HEADS, HD).astype(jnp.float32)
    query_f32 = query_row.reshape(block_count, BLOCK, HEADS, HD).astype(jnp.float32)
    scores = jnp.einsum('bqhd,bkhd->bhqk', query_f32, key_part) * (HD ** -0.5)
    key_mask = jnp.repeat(usable, BLOCK, axis=1)[:, None, None, :]
    scores = jnp.where(key_mask, scores, -jnp.inf)
    row_top = jnp.max(scores, axis=-1, keepdims=True)
    weights = jnp.exp(scores - row_top)
    denominator = jnp.sum(weights, axis=-1)
    rounded = lax.optimization_barrier(weights.astype(jnp.bfloat16))
    mixture = jnp.einsum('bhqk,bkhd->bqhd', rounded.astype(jnp.float32), value_part)
    mixture = mixture / jnp.transpose(denominator, (0, 2, 1))[..., None]
    return mixture.reshape(NLON, HEADS * HD).astype(jnp.bfloat16)


def band_gram(band_rows):
    flat_rows = band_rows.astype(jnp.float32)
    return jnp.einsum('nhd,nhe->hde', flat_rows, flat_rows)


def reference(queries, keyval, keep, lists):
    attended = lax.map(lambda lat_row: row_attention(lat_row, queries, keyval, keep, lists), jnp.arange(NLAT, dtype=jnp.int32))
    bands = attended.reshape(N_LAT, TLAT * NLON, HEADS, HD)
    gram_factor = lax.map(band_gram, bands)
    return attended, gram_factor
```

```python
import functools

import jax
import jax.numpy as jnp
from jax import lax
from jax.experimental import pallas as pl
from jax.experimental.pallas import tpu as pltpu
from jax.sharding import PartitionSpec as P

HEADS = 16
HD = 128
BLOCK = 32
HALO = 2
CAND = 15
NB = 13
ROWS = 40
NEG = -1e30
LOG2 = 1.4426950408889634 * HD ** (-0.5)

VMEM = pl.BlockSpec(memory_space=pltpu.VMEM)
SMEM = pl.BlockSpec(memory_space=pltpu.SMEM)


def iota(shape, axis):
    return lax.broadcasted_iota(jnp.int32, shape, axis)


def prepare_body(rows_total, lat_ref, keep_ref, lists_ref, q_ref, west_ref, east_ref, own_ref):
    first = lat_ref[0] * 2
    lane = iota((1, 128), 1)
    for b, out in ((0, west_ref), (1, east_ref)):
        for t in range(2):
            listed = jnp.zeros((1, 128), jnp.int32)
            for n in range(NB):
                listed = jnp.where(lane == lists_ref[t, b, n], 1, listed)
            usable = jnp.zeros((1, 128), jnp.int32)
            for k in range(2 * HALO + 1):
                row = first + (t + k - HALO)
                inside = jnp.logical_and(row >= 0, row < rows_total)
                if k == HALO:
                    good = 1
                else:
                    good = jnp.where(inside, keep_ref[jnp.clip(row, 0, rows_total - 1)], 0)
                usable = jnp.where((lane >= 3 * k) & (lane < 3 * k + 3), good, usable)
            seen = jnp.where((listed == 1) & (usable == 1), 1.0, 0.0)
            seen = jnp.broadcast_to(seen, (BLOCK, 128)).astype(jnp.bfloat16)
            out[HEADS, t * BLOCK : (t + 1) * BLOCK, :] = seen
            own_ref[b, t * BLOCK : (t + 1) * BLOCK, :] = seen
            for h in range(HEADS):
                out[h, t * BLOCK : (t + 1) * BLOCK, :] = q_ref[
                    t, b * BLOCK : (b + 1) * BLOCK, h * HD : (h + 1) * HD
                ]


def bias_of(seen, t, b, key_blocks):
    width = len(key_blocks) * BLOCK
    cand = iota((128, 6 * width), 0)
    key = iota((128, 6 * width), 1)
    hit = jnp.zeros((128, 6 * width), jnp.bool_)
    for row in range(6):
        if 0 <= row - t <= 4:
            for n, kb in enumerate(key_blocks):
                if -1 <= kb - b <= 1:
                    c = 3 * (row - t) + (kb - b) + 1
                    low = row * width + n * BLOCK
                    hit = hit | ((cand == c) & (key >= low) & (key < low + BLOCK))
    spread = jnp.where(hit, 1.0, 0.0).astype(jnp.bfloat16)
    shown = jnp.dot(seen, spread, preferred_element_type=jnp.float32)
    return jnp.where(shown > 0.5, 0.0, NEG)


def rows_of(refs, part, blocks, h):
    cells = slice(blocks[0] * BLOCK, (blocks[-1] + 1) * BLOCK)
    return jnp.concatenate(
        [ref[part, r, cells, h * HD : (h + 1) * HD] for ref in refs for r in range(2)], axis=0
    )


def attend(q, keys, values, bias):
    scores = lax.dot_general(q, keys, (((1,), (1,)), ((), ())), preferred_element_type=jnp.float32)
    scores = scores * LOG2 + bias
    top = jnp.max(scores, axis=-1, keepdims=True)
    weights = jnp.exp2(scores - top)
    total = jnp.sum(weights, axis=-1, keepdims=True)
    mixed = jnp.dot(weights.astype(jnp.bfloat16), values, preferred_element_type=jnp.float32)
    return (mixed / total).astype(jnp.bfloat16), top + jnp.log2(total)


def remote_body(west_ref, east_ref, low_ref, own_ref, high_ref, to_west_ref, to_east_ref):
    refs = (low_ref, own_ref, high_ref)
    lane = iota((2 * BLOCK, 128), 1)
    for q_ref, out, b, kb, held in ((west_ref, to_west_ref, 1, 2, 0), (east_ref, to_east_ref, 0, -1, 1)):
        bias = jnp.concatenate(
            [bias_of(q_ref[HEADS, t * BLOCK : (t + 1) * BLOCK, :], t, b, (kb,)) for t in range(2)], axis=0
        )
        stats = jnp.zeros((2 * BLOCK, 128), jnp.float32)
        for h in range(HEADS):
            mixed, level = attend(
                q_ref[h], rows_of(refs, 0, (held,), h), rows_of(refs, 1, (held,), h), bias
            )
            out[h] = mixed
            stats = jnp.where(lane == h, level, stats)
        coarse = stats.astype(jnp.bfloat16).astype(jnp.float32)
        rest = stats - coarse
        middle = rest.astype(jnp.bfloat16).astype(jnp.float32)
        fine = rest - middle
        packed = coarse + pltpu.roll(middle, HEADS, 1) + pltpu.roll(fine, 2 * HEADS, 1)
        out[HEADS] = packed.astype(jnp.bfloat16)


def own_body(q_ref, seen_ref, low_ref, own_ref, high_ref, out_ref, level_ref):
    refs = (low_ref, own_ref, high_ref)
    lane = iota((4 * BLOCK, 128), 1)
    bias = jnp.concatenate(
        [
            bias_of(seen_ref[b, t * BLOCK : (t + 1) * BLOCK, :], t, b, (0, 1))
            for b in range(2)
            for t in range(2)
        ],
        axis=0,
    )
    stats = jnp.zeros((4 * BLOCK, 128), jnp.float32)
    for h in range(HEADS):
        q = jnp.concatenate(
            [
                q_ref[t, b * BLOCK : (b + 1) * BLOCK, h * HD : (h + 1) * HD]
                for b in range(2)
                for t in range(2)
            ],
            axis=0,
        )
        mixed, level = attend(q, rows_of(refs, 0, (0, 1), h), rows_of(refs, 1, (0, 1), h), bias)
        out_ref[h] = mixed
        stats = jnp.where(lane == h, level, stats)
    level_ref[...] = stats


def combine_body(own_ref, level_ref, west_ref, east_ref, out_ref, packed_ref):
    mine, theirs = [], []
    for b, ref in ((0, west_ref), (1, east_ref)):
        split = ref[HEADS].astype(jnp.float32)
        far = split + pltpu.roll(split, 128 - HEADS, 1) + pltpu.roll(split, 128 - 2 * HEADS, 1)
        near = level_ref[b * 2 * BLOCK : (b + 1) * 2 * BLOCK, :]
        top = jnp.maximum(near, far)
        near, far = jnp.exp2(near - top), jnp.exp2(far - top)
        both = near + far
        mine.append(near / both)
        theirs.append(far / both)
    row, lane = iota((64, 128), 0), iota((64, 128), 1)
    for h in range(HEADS):
        parts = []
        for b, ref in ((0, west_ref), (1, east_ref)):
            near = own_ref[h, b * 2 * BLOCK : (b + 1) * 2 * BLOCK, :].astype(jnp.float32)
            far = ref[h].astype(jnp.float32)
            part = (near * mine[b][:, h : h + 1] + far * theirs[b][:, h : h + 1]).astype(jnp.bfloat16)
            for t in range(2):
                out_ref[t, b * BLOCK : (b + 1) * BLOCK, h * HD : (h + 1) * HD] = part[
                    t * BLOCK : (t + 1) * BLOCK
                ]
            parts.append(part)
        cells = jnp.concatenate(parts, axis=0)
        gram = lax.dot_general(cells, cells, (((0,), (0,)), ((), ())), preferred_element_type=jnp.float32)
        upper, lower = gram[:64], gram[64:]
        folded = jnp.where((lane < 64) & (row > lane), pltpu.roll(lower, 64, 1), upper).astype(jnp.bfloat16)
        diagonal = jnp.sum(jnp.where(lane - 64 == row, lower, 0.0), axis=0, keepdims=True)
        diagonal = jnp.broadcast_to(diagonal, (8, 128)).astype(jnp.bfloat16)
        for half in range(2):
            packed_ref[2 * h + half, :32, :] = folded[half * 32 : (half + 1) * 32]
            packed_ref[2 * h + half, 32:, :] = diagonal


def sum_body(x_ref, out_ref):
    total = jnp.sum(x_ref[...].astype(jnp.float32), axis=0).astype(jnp.bfloat16)
    out_ref[...] = jnp.broadcast_to(total[None], out_ref.shape)


def unpack_body(x_ref, out_ref):
    row, lane = iota((64, 128), 0), iota((64, 128), 1)
    for h in range(HEADS):
        folded = jnp.concatenate([x_ref[2 * h, :32, :], x_ref[2 * h + 1, :32, :]], axis=0).astype(jnp.float32)
        diagonal = x_ref[2 * h, 32:, :].astype(jnp.float32)[:1]
        turned = jnp.concatenate([folded, jnp.zeros_like(folded)], axis=0).T
        out_ref[0, h, :64, :] = jnp.where((lane < 64) & (row > lane), turned[:64], folded)
        corner = pltpu.roll(jnp.where(row > lane, folded, turned[:64]), 64, 1)
        corner = jnp.where(lane - 64 == row, diagonal, corner)
        out_ref[0, h, 64:, :] = jnp.where(lane < 64, turned[64:], corner)


def call(body, outs, specs, flops=0, moved=0, name=None):
    return pl.pallas_call(
        body,
        out_shape=[jax.ShapeDtypeStruct(shape, dtype) for shape, dtype in outs],
        in_specs=specs,
        out_specs=[VMEM] * len(outs),
        compiler_params=pltpu.CompilerParams(vmem_limit_bytes=40 << 20),
        cost_estimate=pl.CostEstimate(flops=flops, bytes_accessed=moved, transcendentals=0),
        name=name,
    )


def local(queries, keyval, keep, lists):
    bf16, f32 = jnp.bfloat16, jnp.float32
    lats, lons = lax.axis_size("lat"), lax.axis_size("lon")
    up = [(i, i + 1) for i in range(lats - 1)]
    down = [(i + 1, i) for i in range(lats - 1)]
    east = [(i, (i + 1) % lons) for i in range(lons)]
    west = [(i, (i - 1) % lons) for i in range(lons)]
    edge = ((HEADS + 1, 2 * BLOCK, HD), bf16)

    low = lax.ppermute(keyval, "lat", up)
    high = lax.ppermute(keyval, "lat", down)
    lat = lax.axis_index("lat").astype(jnp.int32).reshape(1)
    to_west, to_east, seen = call(
        functools.partial(prepare_body, 2 * lats),
        [edge, edge, ((2, 2 * BLOCK, 128), bf16)],
        [SMEM, SMEM, SMEM, VMEM],
        moved=1 << 20,
        name="prepare",
    )(lat, keep, lists, queries)
    from_west = lax.ppermute(to_east, "lon", east)
    from_east = lax.ppermute(to_west, "lon", west)
    back_west, back_east = call(
        remote_body, [edge, edge], [VMEM] * 5, flops=1 << 29, moved=4 << 20, name="remote"
    )(from_west, from_east, low, keyval, high)
    part_east = lax.ppermute(back_west, "lon", west)
    part_west = lax.ppermute(back_east, "lon", east)
    own, level = call(
        own_body,
        [((HEADS, 4 * BLOCK, HD), bf16), ((4 * BLOCK, 128), f32)],
        [VMEM] * 5,
        flops=1 << 30,
        moved=4 << 20,
        name="own",
    )(queries, seen, low, keyval, high)
    attended, packed = call(
        combine_body,
        [(queries.shape, bf16), ((2 * HEADS, ROWS, 128), bf16)],
        [VMEM] * 4,
        name="combine",
    )(own, level, part_west, part_east)
    swapped = lax.all_to_all(packed, "lon", 0, 0, tiled=True)
    (summed,) = call(sum_body, [((2 * HEADS, ROWS, 128), bf16)], [VMEM], name="total")(swapped)
    gathered = lax.all_to_all(summed, "lon", 0, 0, tiled=True)
    (gram,) = call(unpack_body, [((1, HEADS, HD, HD), f32)], [VMEM], name="unpack")(gathered)
    return attended, gram


def solution(mesh):
    placed = (P("lat", "lon", None), P(None, "lat", "lon", None), P(), P("lat", "lon", None))
    return jax.shard_map(
        local,
        mesh=mesh,
        in_specs=placed,
        out_specs=(P("lat", "lon", None), P("lat", None, None, None)),
        check_vma=False,
    )
```

```python
import functools

import jax
import jax.numpy as jnp
from jax import lax
from jax.experimental import pallas as pl
from jax.experimental.pallas import tpu as pltpu
from jax.sharding import PartitionSpec as P

HEADS = 16
HD = 128
BLOCK = 32
HALO = 2
CAND = 15
NB = 13
ROWS = 40
NEG = -1e30
LOG2 = 1.4426950408889634 * HD ** (-0.5)

VMEM = pl.BlockSpec(memory_space=pltpu.VMEM)
SMEM = pl.BlockSpec(memory_space=pltpu.SMEM)
HBM = pl.BlockSpec(memory_space=pltpu.HBM)
ANY = pl.BlockSpec(memory_space=pl.ANY)


def iota(shape, axis):
    return lax.broadcasted_iota(jnp.int32, shape, axis)


def place(lat_ref, lon_ref):
    return lax.rem(lat_ref[0], 2), lax.rem(lon_ref[0], 2)


def prepare_body(rows_total, lat_ref, lon_ref, keep_hbm, lists_hbm, q_hbm, out0_ref, out1_ref, keep_ref, lists_ref, q_ref, sems):
    copies = [
        pltpu.make_async_copy(src, dst, sems.at[i])
        for i, (src, dst) in enumerate(((lists_hbm, lists_ref), (keep_hbm, keep_ref), (q_hbm, q_ref)))
    ]
    for copy in copies:
        copy.start()
    first = lat_ref[0] * 2
    _, odd = place(lat_ref, lon_ref)
    lane = iota((1, 128), 1)
    copies[0].wait()
    copies[1].wait()
    for b, out in ((1 - odd, out0_ref), (odd, out1_ref)):
        for t in range(2):
            listed = jnp.zeros((1, 128), jnp.int32)
            for n in range(NB):
                listed = jnp.where(lane == lists_ref[t, b, n], 1, listed)
            usable = jnp.zeros((1, 128), jnp.int32)
            for k in range(2 * HALO + 1):
                row = first + (t + k - HALO)
                inside = jnp.logical_and(row >= 0, row < rows_total)
                if k == HALO:
                    good = 1
                else:
                    good = jnp.where(inside, keep_ref[jnp.clip(row, 0, rows_total - 1)], 0)
                usable = jnp.where((lane >= 3 * k) & (lane < 3 * k + 3), good, usable)
            seen = jnp.where((listed == 1) & (usable == 1), 1.0, 0.0)
            seen = jnp.broadcast_to(seen, (BLOCK, 128)).astype(jnp.bfloat16)
            out[HEADS, t * BLOCK : (t + 1) * BLOCK, :] = seen
    copies[2].wait()
    for b, out in ((1 - odd, out0_ref), (odd, out1_ref)):
        cells = pl.ds(pl.multiple_of(b * BLOCK, BLOCK), BLOCK)
        for t in range(2):
            for h in range(HEADS):
                out[h, t * BLOCK : (t + 1) * BLOCK, :] = q_ref[t, cells, h * HD : (h + 1) * HD]


def hold_body(x_ref, after_ref, out_ref):
    del after_ref
    out_ref[...] = x_ref[...]


def bias_of(seen, t, lat_odd, blocks, step):
    shape = (128, 6 * blocks * BLOCK)
    cand, key = iota(shape, 0), iota(shape, 1)
    slot = key // (blocks * BLOCK)
    row = slot + jnp.where(slot < 2, 4 * lat_odd, jnp.where(slot < 4, 0, -4 * lat_odd)) - t
    step = step + (key // BLOCK) % blocks
    inside = (row >= 0) & (row <= 2 * HALO) & (step >= -1) & (step <= 1)
    spread = jnp.where(inside & (cand == 3 * row + step + 1), 1.0, 0.0).astype(jnp.bfloat16)
    shown = jnp.dot(seen, spread, preferred_element_type=jnp.float32)
    return jnp.where(shown > 0.5, 0.0, NEG)


def rows_of(refs, part, cells, h):
    return jnp.concatenate(
        [ref[part, r, cells, h * HD : (h + 1) * HD] for ref in refs for r in range(2)], axis=0
    )


def scores_of(q, keys):
    return lax.dot_general(q, keys, (((1,), (1,)), ((), ())), preferred_element_type=jnp.float32)


def staged(*stages):
    held = [{} for _ in stages]
    for step in range(HEADS + len(stages) - 1):
        for i, stage in enumerate(stages):
            h = step - i
            if 0 <= h < HEADS:
                held[i][h] = stage(h) if i == 0 else stage(h, held[i - 1].pop(h))


def softmax_stage(bias, stats):
    lane = iota(bias.shape[:1] + (128,), 1)

    def stage(h, scores):
        scores = scores * LOG2 + bias
        top = jnp.max(scores, axis=-1, keepdims=True)
        weights = jnp.exp2(scores - top)
        total = jnp.sum(weights, axis=-1, keepdims=True)
        stats[0] = jnp.where(lane == h, top, stats[0])
        stats[1] = jnp.where(lane == h, total, stats[1])
        return weights.astype(jnp.bfloat16)

    return stage


def own_body(lat_ref, lon_ref, q0_ref, q1_ref, far_ref, own_ref, near_ref, after_ref, out_ref, top_ref, total_ref):
    del after_ref
    refs = (far_ref, own_ref, near_ref)
    lat_odd, odd = place(lat_ref, lon_ref)
    cells = slice(0, 2 * BLOCK)
    bias = jnp.concatenate(
        [
            bias_of(ref[HEADS, t * BLOCK : (t + 1) * BLOCK, :], t, lat_odd, 2, -b)
            for b, ref in ((1 - odd, q0_ref), (odd, q1_ref))
            for t in range(2)
        ],
        axis=0,
    )
    stats = [jnp.zeros((4 * BLOCK, 128), jnp.float32), jnp.ones((4 * BLOCK, 128), jnp.float32)]

    def score(h):
        return scores_of(jnp.concatenate([q0_ref[h], q1_ref[h]], axis=0), rows_of(refs, 0, cells, h))

    def mix(h, weights):
        mixed = jnp.dot(weights, rows_of(refs, 1, cells, h), preferred_element_type=jnp.float32)
        out_ref[h] = mixed.astype(jnp.bfloat16)

    staged(score, softmax_stage(bias, stats), mix)
    top_ref[...] = stats[0]
    total_ref[...] = stats[1]


def thirds(x):
    coarse = x.astype(jnp.bfloat16).astype(jnp.float32)
    rest = x - coarse
    middle = rest.astype(jnp.bfloat16).astype(jnp.float32)
    return coarse, middle, rest - middle


def remote_body(partner, lat_ref, lon_ref, q_ref, far_ref, own_ref, near_ref, out_ref):
    refs = (far_ref, own_ref, near_ref)
    lat_odd, odd = place(lat_ref, lon_ref)
    held = 1 - odd if partner == 0 else odd
    cells = pl.ds(pl.multiple_of(held * BLOCK, BLOCK), BLOCK)
    bias = jnp.concatenate(
        [
            bias_of(q_ref[HEADS, t * BLOCK : (t + 1) * BLOCK, :], t, lat_odd, 1, 1 - 2 * held)
            for t in range(2)
        ],
        axis=0,
    )
    stats = [jnp.zeros((2 * BLOCK, 128), jnp.float32), jnp.ones((2 * BLOCK, 128), jnp.float32)]

    def score(h):
        return scores_of(q_ref[h], rows_of(refs, 0, cells, h))

    def mix(h, weights):
        mixed = jnp.dot(weights, rows_of(refs, 1, cells, h), preferred_element_type=jnp.float32)
        out_ref[h] = mixed.astype(jnp.bfloat16)

    staged(score, softmax_stage(bias, stats), mix)
    lane = iota((2 * BLOCK, 128), 1)
    packed = jnp.zeros((2 * BLOCK, 128), jnp.float32)
    for i, part in enumerate(thirds(stats[0]) + thirds(stats[1])):
        part = jnp.where(lane < HEADS, part, 0.0)
        packed = packed + (pltpu.roll(part, i * HEADS, 1) if i else part)
    out_ref[HEADS] = packed.astype(jnp.bfloat16)


def combine_body(lon_ref, own_ref, top_ref, total_ref, part0_ref, part1_ref, out_ref, packed_ref):
    half = 2 * BLOCK
    odd = lax.rem(lon_ref[0], 2)
    split = jnp.concatenate([part0_ref[HEADS], part1_ref[HEADS]], axis=0).astype(jnp.float32)
    moved = [split] + [pltpu.roll(split, 128 - i * HEADS, 1) for i in range(1, 6)]
    far_top = moved[0] + moved[1] + moved[2]
    far_total = moved[3] + moved[4] + moved[5]
    lane = iota((4 * BLOCK, 128), 1)
    far_top = jnp.where(lane < HEADS, far_top, 0.0)
    far_total = jnp.where(lane < HEADS, far_total, 1.0)
    near_top = top_ref[...]
    top = jnp.maximum(near_top, far_top)
    mine, theirs = jnp.exp2(near_top - top), jnp.exp2(far_top - top)
    inverse = 1.0 / (mine * total_ref[...] + theirs * far_total)
    mine, theirs = mine * inverse, theirs * inverse
    row, lane = iota((64, 128), 0), iota((64, 128), 1)

    def merge(h):
        far = jnp.concatenate([part0_ref[h], part1_ref[h]], axis=0).astype(jnp.float32)
        near = own_ref[h].astype(jnp.float32)
        cells = (near * mine[:, h : h + 1] + far * theirs[:, h : h + 1]).astype(jnp.bfloat16)
        for i, b in enumerate((1 - odd, odd)):
            place_b = pl.ds(pl.multiple_of(b * BLOCK, BLOCK), BLOCK)
            for t in range(2):
                low = i * half + t * BLOCK
                out_ref[t, place_b, h * HD : (h + 1) * HD] = cells[low : low + BLOCK]
        return cells

    def multiply(h, cells):
        return lax.dot_general(cells, cells, (((0,), (0,)), ((), ())), preferred_element_type=jnp.float32)

    def pack(h, gram):
        upper, lower = gram[:64], gram[64:]
        folded = jnp.where((lane < 64) & (row > lane), pltpu.roll(lower, 64, 1), upper).astype(jnp.bfloat16)
        diagonal = jnp.sum(jnp.where(lane - 64 == row, lower, 0.0), axis=0, keepdims=True)
        diagonal = jnp.broadcast_to(diagonal, (8, 128)).astype(jnp.bfloat16)
        for part in range(2):
            packed_ref[2 * h + part, :32, :] = folded[part * 32 : (part + 1) * 32]
            packed_ref[2 * h + part, 32:, :] = diagonal

    staged(merge, multiply, pack)


def sum_body(x_ref, out_ref):
    total = jnp.sum(x_ref[...].astype(jnp.float32), axis=0).astype(jnp.bfloat16)
    out_ref[...] = jnp.broadcast_to(total[None], out_ref.shape)


def unpack_body(x_ref, out_ref):
    row, lane = iota((64, 128), 0), iota((64, 128), 1)
    for h in range(HEADS):
        folded = jnp.concatenate([x_ref[2 * h, :32, :], x_ref[2 * h + 1, :32, :]], axis=0).astype(jnp.float32)
        diagonal = x_ref[2 * h, 32:, :].astype(jnp.float32)[:1]
        turned = jnp.concatenate([folded, jnp.zeros_like(folded)], axis=0).T
        out_ref[0, h, :64, :] = jnp.where((lane < 64) & (row > lane), turned[:64], folded)
        corner = pltpu.roll(jnp.where(row > lane, folded, turned[:64]), 64, 1)
        corner = jnp.where(lane - 64 == row, diagonal, corner)
        out_ref[0, h, 64:, :] = jnp.where(lane < 64, turned[64:], corner)


def call(body, outs, specs, flops=0, moved=0, name=None, scratch=()):
    return pl.pallas_call(
        body,
        out_shape=[jax.ShapeDtypeStruct(shape, dtype) for shape, dtype in outs],
        in_specs=specs,
        out_specs=[VMEM] * len(outs),
        scratch_shapes=scratch,
        compiler_params=pltpu.CompilerParams(vmem_limit_bytes=40 << 20),
        cost_estimate=pl.CostEstimate(flops=flops, bytes_accessed=moved, transcendentals=0),
        name=name,
    )


def local(queries, keyval, keep, lists):
    bf16, f32 = jnp.bfloat16, jnp.float32
    lats, lons = lax.axis_size("lat"), lax.axis_size("lon")
    chips = [(i, i + 1 if i % 2 else i - 1) for i in range(1, lats - 1)]
    cores = [(i, i ^ 1) for i in range(lats)]
    pairs = [(i, i ^ 1) for i in range(lons)], [(i, (i + (1 if i % 2 else -1)) % lons) for i in range(lons)]
    edge = ((HEADS + 1, 2 * BLOCK, HD), bf16)
    level = ((4 * BLOCK, 128), f32)

    far = lax.ppermute(keyval, "lat", chips)
    near = lax.ppermute(keyval, "lat", cores)
    lat = lax.axis_index("lat").astype(jnp.int32).reshape(1)
    lon = lax.axis_index("lon").astype(jnp.int32).reshape(1)
    mine = call(
        functools.partial(prepare_body, 2 * lats),
        [edge, edge],
        [SMEM, SMEM, HBM, HBM, HBM],
        moved=1 << 20,
        name="prepare",
        scratch=[
            pltpu.SMEM(keep.shape, jnp.int32),
            pltpu.SMEM(lists.shape, jnp.int32),
            pltpu.VMEM(queries.shape, bf16),
            pltpu.SemaphoreType.DMA((3,)),
        ],
    )(lat, lon, keep, lists, queries)
    theirs = [lax.ppermute(x, "lon", pair) for x, pair in zip(mine, pairs)]
    (held,) = call(hold_body, [(keyval.shape, bf16)], [VMEM, ANY], moved=2 << 20, name="hold")(keyval, mine[0])
    answers = [
        call(
            functools.partial(remote_body, i),
            [edge],
            [SMEM, SMEM] + [VMEM] * 4,
            flops=1 << 28,
            moved=4 << 20,
            name=f"remote{i}",
        )(lat, lon, theirs[i], far, held, near)[0]
        for i in range(2)
    ]
    parts = [lax.ppermute(x, "lon", pair) for x, pair in zip(answers, pairs)]
    own, top, total = call(
        own_body,
        [((HEADS, 4 * BLOCK, HD), bf16), level, level],
        [SMEM, SMEM] + [VMEM] * 5 + [ANY],
        flops=1 << 29,
        moved=4 << 20,
        name="own",
    )(lat, lon, *mine, far, held, near, answers[1])
    attended, packed = call(
        combine_body,
        [(queries.shape, bf16), ((2 * HEADS, ROWS, 128), bf16)],
        [SMEM] + [VMEM] * 5,
        name="combine",
    )(lon, own, top, total, *parts)
    swapped = lax.all_to_all(packed, "lon", 0, 0, tiled=True)
    (summed,) = call(sum_body, [((2 * HEADS, ROWS, 128), bf16)], [VMEM], name="total")(swapped)
    gathered = lax.all_to_all(summed, "lon", 0, 0, tiled=True)
    (gram,) = call(unpack_body, [((1, HEADS, HD, HD), f32)], [VMEM], name="unpack")(gathered)
    return attended, gram


def solution(mesh):
    placed = (P("lat", "lon", None), P(None, "lat", "lon", None), P(), P("lat", "lon", None))
    return jax.shard_map(
        local,
        mesh=mesh,
        in_specs=placed,
        out_specs=(P("lat", "lon", None), P("lat", None, None, None)),
        check_vma=False,
    )
```

```python
import functools

import jax
import jax.numpy as jnp
from jax import lax
from jax.experimental import pallas as pl
from jax.experimental.pallas import tpu as pltpu
from jax.sharding import PartitionSpec as P

HEADS = 16
HD = 128
BLOCK = 32
HALO = 2
CAND = 15
NB = 13
ROWS = 32
NEG = -1e30
COPIED = 4
OWN_GROUP, REMOTE_GROUP, COMBINE_GROUP = 1, 8, 8
LOG2 = 1.4426950408889634 * HD ** (-0.5)

VMEM = pl.BlockSpec(memory_space=pltpu.VMEM)
SMEM = pl.BlockSpec(memory_space=pltpu.SMEM)
HBM = pl.BlockSpec(memory_space=pltpu.HBM)
ANY = pl.BlockSpec(memory_space=pl.ANY)


def iota(shape, axis):
    return lax.broadcasted_iota(jnp.int32, shape, axis)


def place(lat_ref, lon_ref):
    return lax.rem(lat_ref[0], 2), lax.rem(lon_ref[0], 2)


def prepare_body(rows_total, lat_ref, lon_ref, keep_hbm, lists_hbm, q_hbm, out0_ref, out1_ref, keep_ref, lists_ref, q_ref, sems):
    copies = [
        pltpu.make_async_copy(src, dst, sems.at[i])
        for i, (src, dst) in enumerate(((lists_hbm, lists_ref), (keep_hbm, keep_ref), (q_hbm, q_ref)))
    ]
    for copy in copies:
        copy.start()
    first = lat_ref[0] * 2
    _, odd = place(lat_ref, lon_ref)
    lane = iota((1, 128), 1)
    copies[0].wait()
    copies[1].wait()
    for b, out in ((odd, out0_ref), (1 - odd, out1_ref)):
        for t in range(2):
            listed = jnp.zeros((1, 128), jnp.int32)
            for n in range(NB):
                listed = jnp.where(lane == lists_ref[t, b, n], 1, listed)
            usable = jnp.zeros((1, 128), jnp.int32)
            for k in range(2 * HALO + 1):
                row = first + (t + k - HALO)
                inside = jnp.logical_and(row >= 0, row < rows_total)
                if k == HALO:
                    good = 1
                else:
                    good = jnp.where(inside, keep_ref[jnp.clip(row, 0, rows_total - 1)], 0)
                usable = jnp.where((lane >= 3 * k) & (lane < 3 * k + 3), good, usable)
            seen = jnp.where((listed == 1) & (usable == 1), 1.0, 0.0)
            seen = jnp.broadcast_to(seen, (BLOCK, 128)).astype(jnp.bfloat16)
            out[HEADS, t * BLOCK : (t + 1) * BLOCK, :] = seen
    copies[2].wait()
    for b, out in ((odd, out0_ref), (1 - odd, out1_ref)):
        cells = pl.ds(pl.multiple_of(b * BLOCK, BLOCK), BLOCK)
        for t in range(2):
            for h in range(HEADS):
                out[h, t * BLOCK : (t + 1) * BLOCK, :] = q_ref[t, cells, h * HD : (h + 1) * HD]


def hold_body(x_ref, after_ref, out_ref):
    del after_ref
    out_ref[...] = x_ref[...]


def bias_of(seen, t, lat_odd, blocks, step):
    shape = (128, 6 * blocks * BLOCK)
    cand, key = iota(shape, 0), iota(shape, 1)
    slot = key // (blocks * BLOCK)
    row = slot + jnp.where(slot < 2, 4 * lat_odd, jnp.where(slot < 4, 0, -4 * lat_odd)) - t
    step = step + (key // BLOCK) % blocks
    inside = (row >= 0) & (row <= 2 * HALO) & (step >= -1) & (step <= 1)
    spread = jnp.where(inside & (cand == 3 * row + step + 1), 1.0, 0.0).astype(jnp.bfloat16)
    shown = jnp.dot(seen, spread, preferred_element_type=jnp.float32)
    return jnp.where(shown > 0.5, 0.0, NEG)


def rows_of(refs, part, cells, h):
    return jnp.concatenate(
        [ref[part, r, cells, h * HD : (h + 1) * HD] for ref in refs for r in range(2)], axis=0
    )


def scores_of(q, keys):
    return lax.dot_general(q, keys, (((1,), (1,)), ((), ())), preferred_element_type=jnp.float32)


def staged(group, *stages):
    held = [{} for _ in stages]
    groups = HEADS // group
    for step in range(groups + len(stages) - 1):
        for i, stage in enumerate(stages):
            if 0 <= step - i < groups:
                for h in range((step - i) * group, (step - i + 1) * group):
                    held[i][h] = stage(h) if i == 0 else stage(h, held[i - 1].pop(h))


def softmax_stage(bias, stats):
    lane = iota(bias.shape[:1] + (128,), 1)

    def stage(h, scores):
        scores = scores * LOG2 + bias
        top = jnp.max(scores, axis=-1, keepdims=True)
        weights = jnp.exp2(scores - top)
        total = jnp.sum(weights, axis=-1, keepdims=True)
        stats[0] = jnp.where(lane == h, top, stats[0])
        stats[1] = jnp.where(lane == h, total, stats[1])
        return weights.astype(jnp.bfloat16), 1.0 / total

    return stage


def own_body(lat_ref, lon_ref, q0_ref, q1_ref, far_ref, own_ref, near_ref, after_ref, out_ref, top_ref, total_ref):
    del after_ref
    refs = (far_ref, own_ref, near_ref)
    lat_odd, odd = place(lat_ref, lon_ref)
    cells = slice(0, 2 * BLOCK)
    bias = jnp.concatenate(
        [
            bias_of(ref[HEADS, t * BLOCK : (t + 1) * BLOCK, :], t, lat_odd, 2, -b)
            for b, ref in ((odd, q0_ref), (1 - odd, q1_ref))
            for t in range(2)
        ],
        axis=0,
    )
    stats = [jnp.zeros((4 * BLOCK, 128), jnp.float32), jnp.ones((4 * BLOCK, 128), jnp.float32)]

    def score(h):
        return scores_of(jnp.concatenate([q0_ref[h], q1_ref[h]], axis=0), rows_of(refs, 0, cells, h))

    def mix(h, softmax):
        weights, inverse = softmax
        mixed = jnp.dot(weights, rows_of(refs, 1, cells, h), preferred_element_type=jnp.float32)
        out_ref[h] = (mixed * inverse).astype(jnp.bfloat16)

    staged(OWN_GROUP, score, softmax_stage(bias, stats), mix)
    top_ref[...] = stats[0]
    total_ref[...] = stats[1]


def thirds(x):
    coarse = x.astype(jnp.bfloat16).astype(jnp.float32)
    rest = x - coarse
    middle = rest.astype(jnp.bfloat16).astype(jnp.float32)
    return coarse, middle, rest - middle


def remote_body(partner, lat_ref, lon_ref, q_ref, far_ref, own_ref, near_ref, out_ref):
    refs = (far_ref, own_ref, near_ref)
    lat_odd, odd = place(lat_ref, lon_ref)
    held = odd if partner == 0 else 1 - odd
    cells = pl.ds(pl.multiple_of(held * BLOCK, BLOCK), BLOCK)
    bias = jnp.concatenate(
        [
            bias_of(q_ref[HEADS, t * BLOCK : (t + 1) * BLOCK, :], t, lat_odd, 1, 1 - 2 * held)
            for t in range(2)
        ],
        axis=0,
    )
    stats = [jnp.zeros((2 * BLOCK, 128), jnp.float32), jnp.ones((2 * BLOCK, 128), jnp.float32)]

    def score(h):
        return scores_of(q_ref[h], rows_of(refs, 0, cells, h))

    def mix(h, softmax):
        weights, inverse = softmax
        mixed = jnp.dot(weights, rows_of(refs, 1, cells, h), preferred_element_type=jnp.float32)
        out_ref[h] = (mixed * inverse).astype(jnp.bfloat16)

    staged(REMOTE_GROUP, score, softmax_stage(bias, stats), mix)
    lane = iota((2 * BLOCK, 128), 1)
    packed = jnp.zeros((2 * BLOCK, 128), jnp.float32)
    for i, part in enumerate(thirds(stats[0]) + thirds(stats[1])):
        part = jnp.where(lane < HEADS, part, 0.0)
        packed = packed + (pltpu.roll(part, i * HEADS, 1) if i else part)
    out_ref[HEADS] = packed.astype(jnp.bfloat16)


def combine_body(lon_ref, own_ref, top_ref, total_ref, part0_ref, part1_ref, out_hbm, packed_ref, diag_ref, out_ref, sems):
    half = 2 * BLOCK
    odd = lax.rem(lon_ref[0], 2)
    split = jnp.concatenate([part0_ref[HEADS], part1_ref[HEADS]], axis=0).astype(jnp.float32)
    moved = [split] + [pltpu.roll(split, 128 - i * HEADS, 1) for i in range(1, 6)]
    far_top = moved[0] + moved[1] + moved[2]
    far_total = moved[3] + moved[4] + moved[5]
    lane = iota((4 * BLOCK, 128), 1)
    far_top = jnp.where(lane < HEADS, far_top, 0.0)
    far_total = jnp.where(lane < HEADS, far_total, 1.0)
    near_top = top_ref[...]
    top = jnp.maximum(near_top, far_top)
    mine = jnp.exp2(near_top - top) * total_ref[...]
    theirs = jnp.exp2(far_top - top) * far_total
    share = theirs / (mine + theirs)
    row, lane = iota((64, 128), 0), iota((64, 128), 1)
    pair, side = iota((8, 128), 0), iota((8, 128), 1)
    diagonals = [jnp.zeros((8, 128), jnp.float32)]
    copies = []

    def merge(h):
        far = jnp.concatenate([part0_ref[h], part1_ref[h]], axis=0).astype(jnp.float32)
        near = own_ref[h].astype(jnp.float32)
        cells = (near + (far - near) * share[:, h : h + 1]).astype(jnp.bfloat16)
        for i, b in enumerate((odd, 1 - odd)):
            place_b = pl.ds(pl.multiple_of(b * BLOCK, BLOCK), BLOCK)
            for t in range(2):
                low = i * half + t * BLOCK
                out_ref[t, place_b, h * HD : (h + 1) * HD] = cells[low : low + BLOCK]
        if h % COPIED == COPIED - 1:
            features = slice((h + 1 - COPIED) * HD, (h + 1) * HD)
            copies.append(
                pltpu.make_async_copy(
                    out_ref.at[:, :, features], out_hbm.at[:, :, features], sems.at[h // COPIED]
                )
            )
            copies[-1].start()
        return cells

    def multiply(h, cells):
        return lax.dot_general(cells, cells, (((0,), (0,)), ((), ())), preferred_element_type=jnp.float32)

    def pack(h, gram):
        upper, lower = gram[:64], gram[64:]
        folded = jnp.where((lane < 64) & (row > lane), pltpu.roll(lower, 64, 1), upper).astype(jnp.bfloat16)
        diagonal = jnp.sum(jnp.where(lane - 64 == row, lower, 0.0), axis=0, keepdims=True)
        if h % 2 == 0:
            diagonal = pltpu.roll(diagonal, 64, 1)
        mine_here = (pair == h // 2) & (side // 64 == h % 2)
        diagonals[0] = jnp.where(mine_here, diagonal, diagonals[0])
        for part in range(2):
            packed_ref[2 * h + part] = folded[part * 32 : (part + 1) * 32]

    staged(COMBINE_GROUP, merge, multiply, pack)
    diag_ref[...] = diagonals[0].astype(jnp.bfloat16)
    for copy in copies:
        copy.wait()


def sum_body(x_ref, diag_ref, out_ref):
    total = jnp.sum(x_ref[...].astype(jnp.float32), axis=0).astype(jnp.bfloat16)
    out_ref[:, :ROWS, :] = jnp.broadcast_to(total[None], (2 * HEADS, ROWS, 128))
    out_ref[:, ROWS:, :] = jnp.broadcast_to(diag_ref[...][None], (2 * HEADS, 8, 128))


def unpack_body(x_ref, out_hbm, out_ref, sems):
    row, lane = iota((64, 128), 0), iota((64, 128), 1)
    odd_diagonals = jnp.sum(x_ref[:, ROWS:, :].astype(jnp.float32), axis=0)
    even_diagonals = pltpu.roll(odd_diagonals, 64, 1)
    copies = []
    for h in range(HEADS):
        folded = jnp.concatenate([x_ref[2 * h, :ROWS, :], x_ref[2 * h + 1, :ROWS, :]], axis=0).astype(jnp.float32)
        diagonal = (odd_diagonals if h % 2 else even_diagonals)[h // 2 : h // 2 + 1]
        turned = jnp.concatenate([folded, jnp.zeros_like(folded)], axis=0).T
        out_ref[0, h, :64, :] = jnp.where((lane < 64) & (row > lane), turned[:64], folded)
        corner = pltpu.roll(jnp.where(row > lane, folded, turned[:64]), 64, 1)
        corner = jnp.where(lane - 64 == row, diagonal, corner)
        out_ref[0, h, 64:, :] = jnp.where(lane < 64, turned[64:], corner)
        if h % 2:
            pair = pl.ds(h - 1, 2)
            copies.append(pltpu.make_async_copy(out_ref.at[:, pair], out_hbm.at[:, pair], sems.at[h // 2]))
            copies[-1].start()
    for copy in copies:
        copy.wait()


def call(body, outs, specs, flops=0, moved=0, name=None, scratch=(), places=None):
    return pl.pallas_call(
        body,
        out_shape=[jax.ShapeDtypeStruct(shape, dtype) for shape, dtype in outs],
        in_specs=specs,
        out_specs=places or [VMEM] * len(outs),
        scratch_shapes=scratch,
        compiler_params=pltpu.CompilerParams(vmem_limit_bytes=40 << 20),
        cost_estimate=pl.CostEstimate(flops=flops, bytes_accessed=moved, transcendentals=0),
        name=name,
    )


def local(queries, keyval, keep, lists):
    bf16, f32 = jnp.bfloat16, jnp.float32
    lats, lons = lax.axis_size("lat"), lax.axis_size("lon")
    chips = [(i, i + 1 if i % 2 else i - 1) for i in range(1, lats - 1)]
    cores = [(i, i ^ 1) for i in range(lats)]
    pairs = [(i, (i + (1 if i % 2 else -1)) % lons) for i in range(lons)], [(i, i ^ 1) for i in range(lons)]
    edge = ((HEADS + 1, 2 * BLOCK, HD), bf16)
    level = ((4 * BLOCK, 128), f32)

    far = lax.ppermute(keyval, "lat", chips)
    near = lax.ppermute(keyval, "lat", cores)
    lat = lax.axis_index("lat").astype(jnp.int32).reshape(1)
    lon = lax.axis_index("lon").astype(jnp.int32).reshape(1)
    mine = call(
        functools.partial(prepare_body, 2 * lats),
        [edge, edge],
        [SMEM, SMEM, HBM, HBM, HBM],
        moved=1 << 20,
        name="prepare",
        scratch=[
            pltpu.SMEM(keep.shape, jnp.int32),
            pltpu.SMEM(lists.shape, jnp.int32),
            pltpu.VMEM(queries.shape, bf16),
            pltpu.SemaphoreType.DMA((3,)),
        ],
    )(lat, lon, *[pltpu.with_memory_space_constraint(x, pltpu.HBM) for x in (keep, lists, queries)])
    theirs = [lax.ppermute(x, "lon", pair) for x, pair in zip(mine, pairs)]
    (held,) = call(hold_body, [(keyval.shape, bf16)], [VMEM, ANY], moved=2 << 20, name="hold")(keyval, mine[0])
    answers = [
        call(
            functools.partial(remote_body, i),
            [edge],
            [SMEM, SMEM] + [VMEM] * 4,
            flops=1 << 28,
            moved=4 << 20,
            name=f"remote{i}",
        )(lat, lon, theirs[i], far, held, near)[0]
        for i in range(2)
    ]
    parts = [lax.ppermute(x, "lon", pair) for x, pair in zip(answers, pairs)]
    own, top, total = call(
        own_body,
        [((HEADS, 4 * BLOCK, HD), bf16), level, level],
        [SMEM, SMEM] + [VMEM] * 5 + [ANY],
        flops=1 << 29,
        moved=4 << 20,
        name="own",
    )(lat, lon, *mine, far, held, near, answers[1])
    attended, packed, diagonals = call(
        combine_body,
        [(queries.shape, bf16), ((2 * HEADS, ROWS, 128), bf16), ((8, 128), bf16)],
        [SMEM] + [VMEM] * 5,
        name="combine",
        scratch=[pltpu.VMEM(queries.shape, bf16), pltpu.SemaphoreType.DMA((HEADS // COPIED,))],
        places=[HBM, VMEM, VMEM],
    )(lon, own, top, total, *parts)
    swapped = lax.all_to_all(packed, "lon", 0, 0, tiled=True)
    (summed,) = call(sum_body, [((2 * HEADS, ROWS + 8, 128), bf16)], [VMEM] * 2, name="total")(swapped, diagonals)
    gathered = lax.all_to_all(summed, "lon", 0, 0, tiled=True)
    gram_shape = (1, HEADS, HD, HD)
    (gram,) = call(
        unpack_body,
        [(gram_shape, f32)],
        [VMEM],
        name="unpack",
        scratch=[pltpu.VMEM(gram_shape, f32), pltpu.SemaphoreType.DMA((HEADS // 2,))],
        places=[HBM],
    )(gathered)
    return attended, gram


def solution(mesh):
    placed = (P("lat", "lon", None), P(None, "lat", "lon", None), P(), P("lat", "lon", None))
    return jax.shard_map(
        local,
        mesh=mesh,
        in_specs=placed,
        out_specs=(P("lat", "lon", None), P("lat", None, None, None)),
        check_vma=False,
    )
```

```python
import functools

import jax
import jax.numpy as jnp
from jax import lax
from jax.experimental import pallas as pl
from jax.experimental.pallas import tpu as pltpu
from jax.sharding import PartitionSpec as P

HEADS = 16
HD = 128
BLOCK = 32
HALO = 2
CAND = 15
NB = 13
ROWS = 32
NEG = -1e30
COPIED = 4
OWN_GROUP, REMOTE_GROUP, COMBINE_GROUP = 1, 8, 8
LOG2 = 1.4426950408889634 * HD ** (-0.5)

VMEM = pl.BlockSpec(memory_space=pltpu.VMEM)
SMEM = pl.BlockSpec(memory_space=pltpu.SMEM)
HBM = pl.BlockSpec(memory_space=pltpu.HBM)
ANY = pl.BlockSpec(memory_space=pl.ANY)


def iota(shape, axis):
    return lax.broadcasted_iota(jnp.int32, shape, axis)


def place(lat_ref, lon_ref):
    return lax.rem(lat_ref[0], 2), lax.rem(lon_ref[0], 2)


def prepare_body(rows_total, lat_ref, lon_ref, keep_hbm, lists_hbm, q_hbm, out0_ref, out1_ref, keep_ref, lists_ref, q_ref, sems):
    copies = [
        pltpu.make_async_copy(src, dst, sems.at[i])
        for i, (src, dst) in enumerate(((lists_hbm, lists_ref), (keep_hbm, keep_ref), (q_hbm, q_ref)))
    ]
    for copy in copies:
        copy.start()
    first = lat_ref[0] * 2
    _, odd = place(lat_ref, lon_ref)
    lane = iota((1, 128), 1)
    copies[0].wait()
    copies[1].wait()
    for b, out in ((odd, out0_ref), (1 - odd, out1_ref)):
        for t in range(2):
            listed = jnp.zeros((1, 128), jnp.int32)
            for n in range(NB):
                listed = jnp.where(lane == lists_ref[t, b, n], 1, listed)
            usable = jnp.zeros((1, 128), jnp.int32)
            for k in range(2 * HALO + 1):
                row = first + (t + k - HALO)
                inside = jnp.logical_and(row >= 0, row < rows_total)
                if k == HALO:
                    good = 1
                else:
                    good = jnp.where(inside, keep_ref[jnp.clip(row, 0, rows_total - 1)], 0)
                usable = jnp.where((lane >= 3 * k) & (lane < 3 * k + 3), good, usable)
            seen = jnp.where((listed == 1) & (usable == 1), 1.0, 0.0)
            seen = jnp.broadcast_to(seen, (BLOCK, 128)).astype(jnp.bfloat16)
            out[HEADS, t * BLOCK : (t + 1) * BLOCK, :] = seen
    copies[2].wait()
    for b, out in ((odd, out0_ref), (1 - odd, out1_ref)):
        cells = pl.ds(pl.multiple_of(b * BLOCK, BLOCK), BLOCK)
        for t in range(2):
            for h in range(HEADS):
                out[h, t * BLOCK : (t + 1) * BLOCK, :] = q_ref[t, cells, h * HD : (h + 1) * HD]


def hold_body(x_ref, after_ref, out_ref):
    del after_ref
    out_ref[...] = x_ref[...]


def bias_of(seen, t, lat_odd, blocks, step):
    shape = (128, 6 * blocks * BLOCK)
    cand, key = iota(shape, 0), iota(shape, 1)
    slot = key // (blocks * BLOCK)
    row = slot + jnp.where(slot < 2, 4 * lat_odd, jnp.where(slot < 4, 0, -4 * lat_odd)) - t
    step = step + (key // BLOCK) % blocks
    inside = (row >= 0) & (row <= 2 * HALO) & (step >= -1) & (step <= 1)
    spread = jnp.where(inside & (cand == 3 * row + step + 1), 1.0, 0.0).astype(jnp.bfloat16)
    shown = jnp.dot(seen, spread, preferred_element_type=jnp.float32)
    return jnp.where(shown > 0.5, 0.0, NEG)


def rows_of(refs, part, cells, h):
    return jnp.concatenate(
        [ref[part, r, cells, h * HD : (h + 1) * HD] for ref in refs for r in range(2)], axis=0
    )


def scores_of(q, keys):
    return lax.dot_general(q, keys, (((1,), (1,)), ((), ())), preferred_element_type=jnp.float32)


def staged(group, *stages):
    held = [{} for _ in stages]
    groups = HEADS // group
    for step in range(groups + len(stages) - 1):
        for i, stage in enumerate(stages):
            if 0 <= step - i < groups:
                for h in range((step - i) * group, (step - i + 1) * group):
                    held[i][h] = stage(h) if i == 0 else stage(h, held[i - 1].pop(h))


def softmax_stage(bias, stats):
    lane = iota(bias.shape[:1] + (128,), 1)

    def stage(h, scores):
        scores = scores * LOG2 + bias
        top = jnp.max(scores, axis=-1, keepdims=True)
        weights = jnp.exp2(scores - top)
        total = jnp.sum(weights, axis=-1, keepdims=True)
        stats[0] = jnp.where(lane == h, top, stats[0])
        stats[1] = jnp.where(lane == h, total, stats[1])
        return weights.astype(jnp.bfloat16), 1.0 / total

    return stage


def own_body(lat_ref, lon_ref, q0_ref, q1_ref, far_ref, own_ref, near_ref, after_ref, out_ref, top_ref, total_ref):
    del after_ref
    refs = (far_ref, own_ref, near_ref)
    lat_odd, odd = place(lat_ref, lon_ref)
    cells = slice(0, 2 * BLOCK)
    bias = jnp.concatenate(
        [
            bias_of(ref[HEADS, t * BLOCK : (t + 1) * BLOCK, :], t, lat_odd, 2, -b)
            for b, ref in ((odd, q0_ref), (1 - odd, q1_ref))
            for t in range(2)
        ],
        axis=0,
    )
    stats = [jnp.zeros((4 * BLOCK, 128), jnp.float32), jnp.ones((4 * BLOCK, 128), jnp.float32)]

    def score(h):
        return scores_of(jnp.concatenate([q0_ref[h], q1_ref[h]], axis=0), rows_of(refs, 0, cells, h))

    def mix(h, softmax):
        weights, inverse = softmax
        mixed = jnp.dot(weights, rows_of(refs, 1, cells, h), preferred_element_type=jnp.float32)
        out_ref[h] = (mixed * inverse).astype(jnp.bfloat16)

    staged(OWN_GROUP, score, softmax_stage(bias, stats), mix)
    top_ref[...] = stats[0]
    total_ref[...] = stats[1]


def thirds(x):
    coarse = x.astype(jnp.bfloat16).astype(jnp.float32)
    rest = x - coarse
    middle = rest.astype(jnp.bfloat16).astype(jnp.float32)
    return coarse, middle, rest - middle


def remote_body(partner, lat_ref, lon_ref, q_ref, far_ref, own_ref, near_ref, out_ref):
    refs = (far_ref, own_ref, near_ref)
    lat_odd, odd = place(lat_ref, lon_ref)
    held = odd if partner == 0 else 1 - odd
    cells = pl.ds(pl.multiple_of(held * BLOCK, BLOCK), BLOCK)
    bias = jnp.concatenate(
        [
            bias_of(q_ref[HEADS, t * BLOCK : (t + 1) * BLOCK, :], t, lat_odd, 1, 1 - 2 * held)
            for t in range(2)
        ],
        axis=0,
    )
    stats = [jnp.zeros((2 * BLOCK, 128), jnp.float32), jnp.ones((2 * BLOCK, 128), jnp.float32)]

    def score(h):
        return scores_of(q_ref[h], rows_of(refs, 0, cells, h))

    def mix(h, softmax):
        weights, inverse = softmax
        mixed = jnp.dot(weights, rows_of(refs, 1, cells, h), preferred_element_type=jnp.float32)
        out_ref[h] = (mixed * inverse).astype(jnp.bfloat16)

    staged(REMOTE_GROUP, score, softmax_stage(bias, stats), mix)
    lane = iota((2 * BLOCK, 128), 1)
    packed = jnp.zeros((2 * BLOCK, 128), jnp.float32)
    for i, part in enumerate(thirds(stats[0]) + thirds(stats[1])):
        part = jnp.where(lane < HEADS, part, 0.0)
        packed = packed + (pltpu.roll(part, i * HEADS, 1) if i else part)
    out_ref[HEADS] = packed.astype(jnp.bfloat16)


def share_of(part_ref, top, total):
    split = part_ref[HEADS].astype(jnp.float32)
    moved = [split] + [pltpu.roll(split, 128 - i * HEADS, 1) for i in range(1, 6)]
    lane = iota((2 * BLOCK, 128), 1)
    far_top = jnp.where(lane < HEADS, moved[0] + moved[1] + moved[2], 0.0)
    far_total = jnp.where(lane < HEADS, moved[3] + moved[4] + moved[5], 1.0)
    highest = jnp.maximum(top, far_top)
    mine = jnp.exp2(top - highest) * total
    theirs = jnp.exp2(far_top - highest) * far_total
    return theirs / (mine + theirs)


def merged(near, far, share):
    near, far = near.astype(jnp.float32), far.astype(jnp.float32)
    return (near + (far - near) * share).astype(jnp.bfloat16)


def merge_body(own_ref, top_ref, total_ref, part_ref, out_ref):
    half = 2 * BLOCK
    share = share_of(part_ref, top_ref[:half], total_ref[:half])
    for h in range(HEADS):
        out_ref[h] = merged(own_ref[h, :half, :], part_ref[h], share[:, h : h + 1])


def combine_body(lon_ref, own_ref, top_ref, total_ref, first_ref, part_ref, out_hbm, packed_ref, diag_ref, out_ref, sems):
    half = 2 * BLOCK
    odd = lax.rem(lon_ref[0], 2)
    share = share_of(part_ref, top_ref[half:], total_ref[half:])
    row, lane = iota((64, 128), 0), iota((64, 128), 1)
    pair, side = iota((8, 128), 0), iota((8, 128), 1)
    diagonals = [jnp.zeros((8, 128), jnp.float32)]
    copies = []

    def merge(h):
        second = merged(own_ref[h, half:, :], part_ref[h], share[:, h : h + 1])
        cells = jnp.concatenate([first_ref[h], second], axis=0)
        for i, b in enumerate((odd, 1 - odd)):
            place_b = pl.ds(pl.multiple_of(b * BLOCK, BLOCK), BLOCK)
            for t in range(2):
                low = i * half + t * BLOCK
                out_ref[t, place_b, h * HD : (h + 1) * HD] = cells[low : low + BLOCK]
        if h % COPIED == COPIED - 1:
            features = slice((h + 1 - COPIED) * HD, (h + 1) * HD)
            copies.append(
                pltpu.make_async_copy(
                    out_ref.at[:, :, features], out_hbm.at[:, :, features], sems.at[h // COPIED]
                )
            )
            copies[-1].start()
        return cells

    def multiply(h, cells):
        return lax.dot_general(cells, cells, (((0,), (0,)), ((), ())), preferred_element_type=jnp.float32)

    def pack(h, gram):
        upper, lower = gram[:64], gram[64:]
        folded = jnp.where((lane < 64) & (row > lane), pltpu.roll(lower, 64, 1), upper).astype(jnp.bfloat16)
        diagonal = jnp.sum(jnp.where(lane - 64 == row, lower, 0.0), axis=0, keepdims=True)
        if h % 2 == 0:
            diagonal = pltpu.roll(diagonal, 64, 1)
        mine_here = (pair == h // 2) & (side // 64 == h % 2)
        diagonals[0] = jnp.where(mine_here, diagonal, diagonals[0])
        for part in range(2):
            packed_ref[2 * h + part] = folded[part * 32 : (part + 1) * 32]

    staged(COMBINE_GROUP, merge, multiply, pack)
    diag_ref[...] = diagonals[0].astype(jnp.bfloat16)
    for copy in copies:
        copy.wait()


def sum_body(x_ref, diag_ref, out_ref):
    total = jnp.sum(x_ref[...].astype(jnp.float32), axis=0).astype(jnp.bfloat16)
    out_ref[:, :ROWS, :] = jnp.broadcast_to(total[None], (2 * HEADS, ROWS, 128))
    out_ref[:, ROWS:, :] = jnp.broadcast_to(diag_ref[...][None], (2 * HEADS, 8, 128))


def unpack_body(x_ref, out_hbm, out_ref, sems):
    row, lane = iota((64, 128), 0), iota((64, 128), 1)
    odd_diagonals = jnp.sum(x_ref[:, ROWS:, :].astype(jnp.float32), axis=0)
    even_diagonals = pltpu.roll(odd_diagonals, 64, 1)
    copies = []
    for h in range(HEADS):
        folded = jnp.concatenate([x_ref[2 * h, :ROWS, :], x_ref[2 * h + 1, :ROWS, :]], axis=0).astype(jnp.float32)
        diagonal = (odd_diagonals if h % 2 else even_diagonals)[h // 2 : h // 2 + 1]
        turned = jnp.concatenate([folded, jnp.zeros_like(folded)], axis=0).T
        out_ref[0, h, :64, :] = jnp.where((lane < 64) & (row > lane), turned[:64], folded)
        corner = pltpu.roll(jnp.where(row > lane, folded, turned[:64]), 64, 1)
        corner = jnp.where(lane - 64 == row, diagonal, corner)
        out_ref[0, h, 64:, :] = jnp.where(lane < 64, turned[64:], corner)
        if h % 2:
            pair = pl.ds(h - 1, 2)
            copies.append(pltpu.make_async_copy(out_ref.at[:, pair], out_hbm.at[:, pair], sems.at[h // 2]))
            copies[-1].start()
    for copy in copies:
        copy.wait()


def call(body, outs, specs, flops=0, moved=0, name=None, scratch=(), places=None):
    return pl.pallas_call(
        body,
        out_shape=[jax.ShapeDtypeStruct(shape, dtype) for shape, dtype in outs],
        in_specs=specs,
        out_specs=places or [VMEM] * len(outs),
        scratch_shapes=scratch,
        compiler_params=pltpu.CompilerParams(vmem_limit_bytes=40 << 20),
        cost_estimate=pl.CostEstimate(flops=flops, bytes_accessed=moved, transcendentals=0),
        name=name,
    )


def local(queries, keyval, keep, lists):
    bf16, f32 = jnp.bfloat16, jnp.float32
    lats, lons = lax.axis_size("lat"), lax.axis_size("lon")
    chips = [(i, i + 1 if i % 2 else i - 1) for i in range(1, lats - 1)]
    cores = [(i, i ^ 1) for i in range(lats)]
    pairs = [(i, (i + (1 if i % 2 else -1)) % lons) for i in range(lons)], [(i, i ^ 1) for i in range(lons)]
    edge = ((HEADS + 1, 2 * BLOCK, HD), bf16)
    level = ((4 * BLOCK, 128), f32)

    far = lax.ppermute(keyval, "lat", chips)
    near = lax.ppermute(keyval, "lat", cores)
    lat = lax.axis_index("lat").astype(jnp.int32).reshape(1)
    lon = lax.axis_index("lon").astype(jnp.int32).reshape(1)
    mine = call(
        functools.partial(prepare_body, 2 * lats),
        [edge, edge],
        [SMEM, SMEM, HBM, HBM, HBM],
        moved=1 << 20,
        name="prepare",
        scratch=[
            pltpu.SMEM(keep.shape, jnp.int32),
            pltpu.SMEM(lists.shape, jnp.int32),
            pltpu.VMEM(queries.shape, bf16),
            pltpu.SemaphoreType.DMA((3,)),
        ],
    )(lat, lon, *[pltpu.with_memory_space_constraint(x, pltpu.HBM) for x in (keep, lists, queries)])
    theirs = [lax.ppermute(x, "lon", pair) for x, pair in zip(mine, pairs)]
    (held,) = call(hold_body, [(keyval.shape, bf16)], [VMEM, ANY], moved=2 << 20, name="hold")(keyval, mine[0])
    answers = [
        call(
            functools.partial(remote_body, i),
            [edge],
            [SMEM, SMEM] + [VMEM] * 4,
            flops=1 << 28,
            moved=4 << 20,
            name=f"remote{i}",
        )(lat, lon, theirs[i], far, held, near)[0]
        for i in range(2)
    ]
    parts = [lax.ppermute(x, "lon", pair) for x, pair in zip(answers, pairs)]
    own, top, total = call(
        own_body,
        [((HEADS, 4 * BLOCK, HD), bf16), level, level],
        [SMEM, SMEM] + [VMEM] * 5 + [ANY],
        flops=1 << 29,
        moved=4 << 20,
        name="own",
    )(lat, lon, *mine, far, held, near, answers[1])
    (first,) = call(merge_body, [((HEADS, 2 * BLOCK, HD), bf16)], [VMEM] * 4, name="merge")(
        own, top, total, parts[0]
    )
    attended, packed, diagonals = call(
        combine_body,
        [(queries.shape, bf16), ((2 * HEADS, ROWS, 128), bf16), ((8, 128), bf16)],
        [SMEM] + [VMEM] * 5,
        name="combine",
        scratch=[pltpu.VMEM(queries.shape, bf16), pltpu.SemaphoreType.DMA((HEADS // COPIED,))],
        places=[HBM, VMEM, VMEM],
    )(lon, own, top, total, first, parts[1])
    swapped = lax.all_to_all(packed, "lon", 0, 0, tiled=True)
    (summed,) = call(sum_body, [((2 * HEADS, ROWS + 8, 128), bf16)], [VMEM] * 2, name="total")(swapped, diagonals)
    gathered = lax.all_to_all(summed, "lon", 0, 0, tiled=True)
    gram_shape = (1, HEADS, HD, HD)
    (gram,) = call(
        unpack_body,
        [(gram_shape, f32)],
        [VMEM],
        name="unpack",
        scratch=[pltpu.VMEM(gram_shape, f32), pltpu.SemaphoreType.DMA((HEADS // 2,))],
        places=[HBM],
    )(gathered)
    return attended, gram


def solution(mesh):
    placed = (P("lat", "lon", None), P(None, "lat", "lon", None), P(), P("lat", "lon", None))
    return jax.shard_map(
        local,
        mesh=mesh,
        in_specs=placed,
        out_specs=(P("lat", "lon", None), P("lat", None, None, None)),
        check_vma=False,
    )
```

```python
import functools

import jax
import jax.numpy as jnp
from jax import lax
from jax.experimental import pallas as pl
from jax.experimental.pallas import tpu as pltpu
from jax.sharding import PartitionSpec as P

HEADS = 16
HD = 128
BLOCK = 32
HALO = 2
CAND = 15
NB = 13
ROWS = 32
NEG = -1e30
COPIED = 4
OWN_GROUP, REMOTE_GROUP, COMBINE_GROUP = 1, 8, 8
LOG2 = 1.4426950408889634 * HD ** (-0.5)

VMEM = pl.BlockSpec(memory_space=pltpu.VMEM)
SMEM = pl.BlockSpec(memory_space=pltpu.SMEM)
HBM = pl.BlockSpec(memory_space=pltpu.HBM)
ANY = pl.BlockSpec(memory_space=pl.ANY)


def iota(shape, axis):
    return lax.broadcasted_iota(jnp.int32, shape, axis)


def place(lat_ref, lon_ref):
    return lax.rem(lat_ref[0], 2), lax.rem(lon_ref[0], 2)


def prepare_body(rows_total, lat_ref, lon_ref, keep_hbm, lists_hbm, q_hbm, out0_ref, out1_ref, keep_ref, lists_ref, q_ref, sems):
    copies = [
        pltpu.make_async_copy(src, dst, sems.at[i])
        for i, (src, dst) in enumerate(((lists_hbm, lists_ref), (keep_hbm, keep_ref)))
    ]
    first = lat_ref[0] * 2
    _, odd = place(lat_ref, lon_ref)
    for i, b in enumerate((odd, 1 - odd)):
        cells = pl.ds(pl.multiple_of(b * BLOCK, BLOCK), BLOCK)
        copies.append(pltpu.make_async_copy(q_hbm.at[:, cells, :], q_ref.at[:, cells, :], sems.at[2 + i]))
    for copy in copies:
        copy.start()
    lane = iota((1, 128), 1)
    copies[0].wait()
    copies[1].wait()
    for b, out in ((odd, out0_ref), (1 - odd, out1_ref)):
        for t in range(2):
            listed = jnp.zeros((1, 128), jnp.int32)
            for n in range(NB):
                listed = jnp.where(lane == lists_ref[t, b, n], 1, listed)
            usable = jnp.zeros((1, 128), jnp.int32)
            for k in range(2 * HALO + 1):
                row = first + (t + k - HALO)
                inside = jnp.logical_and(row >= 0, row < rows_total)
                if k == HALO:
                    good = 1
                else:
                    good = jnp.where(inside, keep_ref[jnp.clip(row, 0, rows_total - 1)], 0)
                usable = jnp.where((lane >= 3 * k) & (lane < 3 * k + 3), good, usable)
            seen = jnp.where((listed == 1) & (usable == 1), 1.0, 0.0)
            seen = jnp.broadcast_to(seen, (BLOCK, 128)).astype(jnp.bfloat16)
            out[HEADS, t * BLOCK : (t + 1) * BLOCK, :] = seen
    for b, out, copy in ((odd, out0_ref, copies[2]), (1 - odd, out1_ref, copies[3])):
        copy.wait()
        cells = pl.ds(pl.multiple_of(b * BLOCK, BLOCK), BLOCK)
        for t in range(2):
            for h in range(HEADS):
                out[h, t * BLOCK : (t + 1) * BLOCK, :] = q_ref[t, cells, h * HD : (h + 1) * HD]


def hold_body(x_ref, after_ref, out_ref):
    del after_ref
    out_ref[...] = x_ref[...]


def bias_of(seen, t, lat_odd, blocks, step):
    shape = (128, 6 * blocks * BLOCK)
    cand, key = iota(shape, 0), iota(shape, 1)
    slot = key // (blocks * BLOCK)
    row = slot + jnp.where(slot < 2, 4 * lat_odd, jnp.where(slot < 4, 0, -4 * lat_odd)) - t
    step = step + (key // BLOCK) % blocks
    inside = (row >= 0) & (row <= 2 * HALO) & (step >= -1) & (step <= 1)
    spread = jnp.where(inside & (cand == 3 * row + step + 1), 1.0, 0.0).astype(jnp.bfloat16)
    shown = jnp.dot(seen, spread, preferred_element_type=jnp.float32)
    return jnp.where(shown > 0.5, 0.0, NEG)


def rows_of(refs, part, cells, h):
    return jnp.concatenate(
        [ref[part, r, cells, h * HD : (h + 1) * HD] for ref in refs for r in range(2)], axis=0
    )


def scores_of(q, keys):
    return lax.dot_general(q, keys, (((1,), (1,)), ((), ())), preferred_element_type=jnp.float32)


def staged(group, *stages):
    held = [{} for _ in stages]
    groups = HEADS // group
    for step in range(groups + len(stages) - 1):
        for i, stage in enumerate(stages):
            if 0 <= step - i < groups:
                for h in range((step - i) * group, (step - i + 1) * group):
                    held[i][h] = stage(h) if i == 0 else stage(h, held[i - 1].pop(h))


def softmax_stage(bias, stats):
    lane = iota(bias.shape[:1] + (128,), 1)

    def stage(h, scores):
        scores = scores * LOG2 + bias
        top = jnp.max(scores, axis=-1, keepdims=True)
        weights = jnp.exp2(scores - top)
        total = jnp.sum(weights, axis=-1, keepdims=True)
        stats[0] = jnp.where(lane == h, top, stats[0])
        stats[1] = jnp.where(lane == h, total, stats[1])
        return weights.astype(jnp.bfloat16), 1.0 / total

    return stage


def own_body(lat_ref, lon_ref, q0_ref, q1_ref, far_ref, own_ref, near_ref, after_ref, out_ref, top_ref, total_ref):
    del after_ref
    refs = (far_ref, own_ref, near_ref)
    lat_odd, odd = place(lat_ref, lon_ref)
    cells = slice(0, 2 * BLOCK)
    bias = jnp.concatenate(
        [
            bias_of(ref[HEADS, t * BLOCK : (t + 1) * BLOCK, :], t, lat_odd, 2, -b)
            for b, ref in ((odd, q0_ref), (1 - odd, q1_ref))
            for t in range(2)
        ],
        axis=0,
    )
    stats = [jnp.zeros((4 * BLOCK, 128), jnp.float32), jnp.ones((4 * BLOCK, 128), jnp.float32)]

    def score(h):
        return scores_of(jnp.concatenate([q0_ref[h], q1_ref[h]], axis=0), rows_of(refs, 0, cells, h))

    def mix(h, softmax):
        weights, inverse = softmax
        mixed = jnp.dot(weights, rows_of(refs, 1, cells, h), preferred_element_type=jnp.float32)
        out_ref[h] = (mixed * inverse).astype(jnp.bfloat16)

    staged(OWN_GROUP, score, softmax_stage(bias, stats), mix)
    top_ref[...] = stats[0]
    total_ref[...] = stats[1]


def thirds(x):
    coarse = x.astype(jnp.bfloat16).astype(jnp.float32)
    rest = x - coarse
    middle = rest.astype(jnp.bfloat16).astype(jnp.float32)
    return coarse, middle, rest - middle


def remote_body(partner, lat_ref, lon_ref, q_ref, far_ref, own_ref, near_ref, out_ref):
    refs = (far_ref, own_ref, near_ref)
    lat_odd, odd = place(lat_ref, lon_ref)
    held = odd if partner == 0 else 1 - odd
    cells = pl.ds(pl.multiple_of(held * BLOCK, BLOCK), BLOCK)
    bias = jnp.concatenate(
        [
            bias_of(q_ref[HEADS, t * BLOCK : (t + 1) * BLOCK, :], t, lat_odd, 1, 1 - 2 * held)
            for t in range(2)
        ],
        axis=0,
    )
    stats = [jnp.zeros((2 * BLOCK, 128), jnp.float32), jnp.ones((2 * BLOCK, 128), jnp.float32)]

    def score(h):
        return scores_of(q_ref[h], rows_of(refs, 0, cells, h))

    def mix(h, softmax):
        weights, inverse = softmax
        mixed = jnp.dot(weights, rows_of(refs, 1, cells, h), preferred_element_type=jnp.float32)
        out_ref[h] = (mixed * inverse).astype(jnp.bfloat16)

    staged(REMOTE_GROUP, score, softmax_stage(bias, stats), mix)
    lane = iota((2 * BLOCK, 128), 1)
    packed = jnp.zeros((2 * BLOCK, 128), jnp.float32)
    for i, part in enumerate(thirds(stats[0]) + thirds(stats[1])):
        part = jnp.where(lane < HEADS, part, 0.0)
        packed = packed + (pltpu.roll(part, i * HEADS, 1) if i else part)
    out_ref[HEADS] = packed.astype(jnp.bfloat16)


def share_of(part_ref, top, total):
    split = part_ref[HEADS].astype(jnp.float32)
    moved = [split] + [pltpu.roll(split, 128 - i * HEADS, 1) for i in range(1, 6)]
    lane = iota((2 * BLOCK, 128), 1)
    far_top = jnp.where(lane < HEADS, moved[0] + moved[1] + moved[2], 0.0)
    far_total = jnp.where(lane < HEADS, moved[3] + moved[4] + moved[5], 1.0)
    highest = jnp.maximum(top, far_top)
    mine = jnp.exp2(top - highest) * total
    theirs = jnp.exp2(far_top - highest) * far_total
    return theirs / (mine + theirs)


def merged(near, far, share):
    near, far = near.astype(jnp.float32), far.astype(jnp.float32)
    return (near + (far - near) * share).astype(jnp.bfloat16)


def merge_body(own_ref, top_ref, total_ref, part_ref, out_ref):
    half = 2 * BLOCK
    share = share_of(part_ref, top_ref[:half], total_ref[:half])
    for h in range(HEADS):
        out_ref[h] = merged(own_ref[h, :half, :], part_ref[h], share[:, h : h + 1])


def combine_body(lon_ref, own_ref, top_ref, total_ref, first_ref, part_ref, out_hbm, packed_ref, diag_ref, out_ref, sems):
    half = 2 * BLOCK
    odd = lax.rem(lon_ref[0], 2)
    share = share_of(part_ref, top_ref[half:], total_ref[half:])
    row, lane = iota((64, 128), 0), iota((64, 128), 1)
    pair, side = iota((8, 128), 0), iota((8, 128), 1)
    diagonals = [jnp.zeros((8, 128), jnp.float32)]
    copies = []

    def merge(h):
        second = merged(own_ref[h, half:, :], part_ref[h], share[:, h : h + 1])
        cells = jnp.concatenate([first_ref[h], second], axis=0)
        for i, b in enumerate((odd, 1 - odd)):
            place_b = pl.ds(pl.multiple_of(b * BLOCK, BLOCK), BLOCK)
            for t in range(2):
                low = i * half + t * BLOCK
                out_ref[t, place_b, h * HD : (h + 1) * HD] = cells[low : low + BLOCK]
        if h % COPIED == COPIED - 1:
            features = slice((h + 1 - COPIED) * HD, (h + 1) * HD)
            copies.append(
                pltpu.make_async_copy(
                    out_ref.at[:, :, features], out_hbm.at[:, :, features], sems.at[h // COPIED]
                )
            )
            copies[-1].start()
        return cells

    def multiply(h, cells):
        return lax.dot_general(cells, cells, (((0,), (0,)), ((), ())), preferred_element_type=jnp.float32)

    def pack(h, gram):
        upper, lower = gram[:64], gram[64:]
        folded = jnp.where((lane < 64) & (row > lane), pltpu.roll(lower, 64, 1), upper).astype(jnp.bfloat16)
        diagonal = jnp.sum(jnp.where(lane - 64 == row, lower, 0.0), axis=0, keepdims=True)
        if h % 2 == 0:
            diagonal = pltpu.roll(diagonal, 64, 1)
        mine_here = (pair == h // 2) & (side // 64 == h % 2)
        diagonals[0] = jnp.where(mine_here, diagonal, diagonals[0])
        for part in range(2):
            packed_ref[2 * h + part] = folded[part * 32 : (part + 1) * 32]

    staged(COMBINE_GROUP, merge, multiply, pack)
    diag_ref[...] = diagonals[0].astype(jnp.bfloat16)
    for copy in copies:
        copy.wait()


def sum_body(x_ref, diag_ref, out_ref):
    total = jnp.sum(x_ref[...].astype(jnp.float32), axis=0).astype(jnp.bfloat16)
    out_ref[:, :ROWS, :] = jnp.broadcast_to(total[None], (2 * HEADS, ROWS, 128))
    out_ref[:, ROWS:, :] = jnp.broadcast_to(diag_ref[...][None], (2 * HEADS, 8, 128))


def unpack_body(x_ref, out_hbm, out_ref, sems):
    row, lane = iota((64, 128), 0), iota((64, 128), 1)
    odd_diagonals = jnp.sum(x_ref[:, ROWS:, :].astype(jnp.float32), axis=0)
    even_diagonals = pltpu.roll(odd_diagonals, 64, 1)
    copies = []
    for h in range(HEADS):
        folded = jnp.concatenate([x_ref[2 * h, :ROWS, :], x_ref[2 * h + 1, :ROWS, :]], axis=0).astype(jnp.float32)
        diagonal = (odd_diagonals if h % 2 else even_diagonals)[h // 2 : h // 2 + 1]
        turned = jnp.concatenate([folded, jnp.zeros_like(folded)], axis=0).T
        out_ref[0, h, :64, :] = jnp.where((lane < 64) & (row > lane), turned[:64], folded)
        corner = pltpu.roll(jnp.where(row > lane, folded, turned[:64]), 64, 1)
        corner = jnp.where(lane - 64 == row, diagonal, corner)
        out_ref[0, h, 64:, :] = jnp.where(lane < 64, turned[64:], corner)
        if h % 2:
            pair = pl.ds(h - 1, 2)
            copies.append(pltpu.make_async_copy(out_ref.at[:, pair], out_hbm.at[:, pair], sems.at[h // 2]))
            copies[-1].start()
    for copy in copies:
        copy.wait()


def call(body, outs, specs, flops=0, moved=0, name=None, scratch=(), places=None):
    return pl.pallas_call(
        body,
        out_shape=[jax.ShapeDtypeStruct(shape, dtype) for shape, dtype in outs],
        in_specs=specs,
        out_specs=places or [VMEM] * len(outs),
        scratch_shapes=scratch,
        compiler_params=pltpu.CompilerParams(vmem_limit_bytes=40 << 20),
        cost_estimate=pl.CostEstimate(flops=flops, bytes_accessed=moved, transcendentals=0),
        name=name,
    )


def local(queries, keyval, keep, lists):
    bf16, f32 = jnp.bfloat16, jnp.float32
    lats, lons = lax.axis_size("lat"), lax.axis_size("lon")
    chips = [(i, i + 1 if i % 2 else i - 1) for i in range(1, lats - 1)]
    cores = [(i, i ^ 1) for i in range(lats)]
    pairs = [(i, (i + (1 if i % 2 else -1)) % lons) for i in range(lons)], [(i, i ^ 1) for i in range(lons)]
    edge = ((HEADS + 1, 2 * BLOCK, HD), bf16)
    level = ((4 * BLOCK, 128), f32)

    far = lax.ppermute(keyval, "lat", chips)
    near = lax.ppermute(keyval, "lat", cores)
    lat = lax.axis_index("lat").astype(jnp.int32).reshape(1)
    lon = lax.axis_index("lon").astype(jnp.int32).reshape(1)
    mine = call(
        functools.partial(prepare_body, 2 * lats),
        [edge, edge],
        [SMEM, SMEM, HBM, HBM, HBM],
        moved=1 << 20,
        name="prepare",
        scratch=[
            pltpu.SMEM(keep.shape, jnp.int32),
            pltpu.SMEM(lists.shape, jnp.int32),
            pltpu.VMEM(queries.shape, bf16),
            pltpu.SemaphoreType.DMA((4,)),
        ],
    )(lat, lon, *[pltpu.with_memory_space_constraint(x, pltpu.HBM) for x in (keep, lists, queries)])
    theirs = [lax.ppermute(x, "lon", pair) for x, pair in zip(mine, pairs)]
    (held,) = call(hold_body, [(keyval.shape, bf16)], [VMEM, ANY], moved=2 << 20, name="hold")(keyval, mine[0])
    answers = [
        call(
            functools.partial(remote_body, i),
            [edge],
            [SMEM, SMEM] + [VMEM] * 4,
            flops=1 << 28,
            moved=4 << 20,
            name=f"remote{i}",
        )(lat, lon, theirs[i], far, held, near)[0]
        for i in range(2)
    ]
    parts = [lax.ppermute(x, "lon", pair) for x, pair in zip(answers, pairs)]
    own, top, total = call(
        own_body,
        [((HEADS, 4 * BLOCK, HD), bf16), level, level],
        [SMEM, SMEM] + [VMEM] * 5 + [ANY],
        flops=1 << 29,
        moved=4 << 20,
        name="own",
    )(lat, lon, *mine, far, held, near, answers[1])
    (first,) = call(merge_body, [((HEADS, 2 * BLOCK, HD), bf16)], [VMEM] * 4, name="merge")(
        own, top, total, parts[0]
    )
    attended, packed, diagonals = call(
        combine_body,
        [(queries.shape, bf16), ((2 * HEADS, ROWS, 128), bf16), ((8, 128), bf16)],
        [SMEM] + [VMEM] * 5,
        name="combine",
        scratch=[pltpu.VMEM(queries.shape, bf16), pltpu.SemaphoreType.DMA((HEADS // COPIED,))],
        places=[HBM, VMEM, VMEM],
    )(lon, own, top, total, first, parts[1])
    swapped = lax.all_to_all(packed, "lon", 0, 0, tiled=True)
    (summed,) = call(sum_body, [((2 * HEADS, ROWS + 8, 128), bf16)], [VMEM] * 2, name="total")(swapped, diagonals)
    gathered = lax.all_to_all(summed, "lon", 0, 0, tiled=True)
    gram_shape = (1, HEADS, HD, HD)
    (gram,) = call(
        unpack_body,
        [(gram_shape, f32)],
        [VMEM],
        name="unpack",
        scratch=[pltpu.VMEM(gram_shape, f32), pltpu.SemaphoreType.DMA((HEADS // 2,))],
        places=[HBM],
    )(gathered)
    return attended, gram


def solution(mesh):
    placed = (P("lat", "lon", None), P(None, "lat", "lon", None), P(), P("lat", "lon", None))
    return jax.shard_map(
        local,
        mesh=mesh,
        in_specs=placed,
        out_specs=(P("lat", "lon", None), P("lat", None, None, None)),
        check_vma=False,
    )
```
